512 devices in a mesh: row: 16 (over y_hi, x, core), col: 32 (over y_lo, z).
Axes of the slice: x: 4, y: 4 (y_hi: 2, y_lo: 2; y = y_hi * 2 + y_lo), z: 16, core: 2. Of those that a mesh axis runs over, the one named last changes fastest.
Arguments:
- inputs: bfloat16 [256, 512, 256], P('row', 'col'), may hold values from -6 to 6
- stored: bfloat16 [256, 512, 256], P('row', 'col'), may hold values from -6 to 6
- upstream: bfloat16 [256, 512, 256], P('row', 'col'), may hold values from -6 to 6
- weight_in: bfloat16 [256, 1024], replicated, may hold values from -0.375 to 0.375
- weight_out: bfloat16 [1024, 256], replicated, may hold values from -0.1875 to 0.1875
- kernel: bfloat16 [27, 27, 256], replicated, may hold values from -0.21875 to 0.21875
Outputs:
- grad_inputs: bfloat16 [256, 512, 256], P('row', 'col')
- grad_weight_in: bfloat16 [256, 1024], replicated
- grad_weight_out: bfloat16 [1024, 256], replicated
- grad_kernel: bfloat16 [27, 27, 256], replicated
The draws below stay inside these ranges and needn't reach their ends.
All inputs are finite; a program needn't handle non-finite values.
Results may differ from the reference program's by a relative error of at most 0.0052.
Values may be sent and summed in bfloat16 or wider, within the bound.
No kernel may reach another device: no remote copies, remote signals or barrier semaphores. Data moves between devices by JAX's collectives and lax.ppermute only.
A program may use at most 64 MiB of HBM per device.

```python
import math
import jax
import jax.numpy as jnp
from jax import lax

C = 256
F = 1024
KS = 27
TH = 16
H = 256
W = 512
TOKENS = 131072


def level_of(rng, extent, split, low, largest):
    factor_of = 1.0
    for position, parts in split:
        draws = jax.random.uniform(jax.random.fold_in(jax.random.fold_in(rng, 6), position), (parts,), jnp.float32, low / len(split), largest / len(split))
        factor_of = factor_of * jnp.repeat(jnp.exp(draws), extent[position] // parts).reshape((-1,) + (1,) * (len(extent) - 1 - position))
    return factor_of


def normal_values(own_key, extent, deviation, limit, cuts=(), held_as=jnp.bfloat16):
    level = level_of(own_key, extent, cuts, -0.22, 0.18) if cuts else 1.0
    values = jax.random.normal(own_key, extent, jnp.float32) * deviation * level
    return jnp.minimum(jnp.maximum(values, -limit), limit).astype(held_as)


def setup_inputs(seed: int = 0) -> dict:
    arg_keys = jax.random.split(jax.random.key(seed), 7)
    return {
        "inputs": normal_values(arg_keys[0], (H, W, C), 1.0, 6.0, ((0, 16), (1, 32))),
        "stored": normal_values(arg_keys[1], (H, W, C), 1.0, 6.0, ((0, 16), (1, 32))),
        "upstream": normal_values(arg_keys[2], (H, W, C), 1.0, 6.0, ((0, 16), (1, 32))),
        "weight_in": normal_values(arg_keys[3], (C, F), C ** -0.5, 0.375),
        "weight_out": normal_values(arg_keys[4], (F, C), F ** -0.5, 0.1875),
        "kernel": normal_values(arg_keys[5], (KS, KS, C), (KS * KS) ** -0.5, 0.21875),
    }


gelu_coef = 0.044715
root_coef = math.sqrt(2.0 / math.pi)

def gelu_parts(values):
    tanh_part = jnp.tanh(root_coef * (values + gelu_coef * values * values * values))
    result = 0.5 * values * (1.0 + tanh_part)
    slopes = 0.5 * (1.0 + tanh_part) + 0.5 * values * (1.0 - tanh_part * tanh_part) * root_coef * (1.0 + 3.0 * gelu_coef * values * values)
    return (result, slopes)

def reference(inputs, stored, upstream, weight_in, weight_out, kernel):
    height, columns, channels = stored.shape
    hidden_units = weight_in.shape[1]
    blocks_z = stored.reshape(height // TH, TH * columns, channels)
    blocks_g = upstream.reshape(height // TH, TH * columns, channels)

    def block_step(state_pair, block_pair):
        stored_block, upstream_block = block_pair
        hidden = jnp.dot(stored_block, weight_in, preferred_element_type=jnp.float32)
        values, slopes = gelu_parts(hidden)
        active = values.astype(jnp.bfloat16)
        back_proj = jnp.dot(upstream_block, weight_out.T, preferred_element_type=jnp.float32)
        grad_hidden = (back_proj * slopes).astype(jnp.bfloat16)
        grad_mid = (upstream_block.astype(jnp.float32) + jnp.dot(grad_hidden, weight_in.T, preferred_element_type=jnp.float32)).astype(jnp.bfloat16)
        sum_in = state_pair[0] + jnp.dot(stored_block.T, grad_hidden, preferred_element_type=jnp.float32)
        sum_out = state_pair[1] + jnp.dot(active.T, upstream_block, preferred_element_type=jnp.float32)
        return ((sum_in, sum_out), grad_mid)
    start = (jnp.zeros((channels, hidden_units), jnp.float32), jnp.zeros((hidden_units, channels), jnp.float32))
    (sum_in, sum_out), mids = lax.scan(block_step, start, (blocks_z, blocks_g))
    grad_mid = mids.reshape(height, columns, channels)
    radius = KS // 2
    full_rows = height + KS - 1
    full_cols = columns + KS - 1
    grad_wide = grad_mid.astype(jnp.float32)
    grad_freq = jnp.fft.rfft2(grad_wide, s=(full_rows, full_cols), axes=(0, 1))
    kernel_freq = jnp.fft.rfft2(kernel.astype(jnp.float32), s=(full_rows, full_cols), axes=(0, 1))
    full_conv = jnp.fft.irfft2(grad_freq * kernel_freq, s=(full_rows, full_cols), axes=(0, 1))
    conv_back = full_conv[radius:radius + height, radius:radius + columns]
    grad_inputs = (grad_wide + conv_back).astype(jnp.bfloat16)
    input_freq = jnp.fft.rfft2(inputs.astype(jnp.float32), s=(full_rows, full_cols), axes=(0, 1))
    correlation = jnp.fft.irfft2(input_freq * jnp.conj(grad_freq), s=(full_rows, full_cols), axes=(0, 1))
    lagged = jnp.roll(correlation, (radius, radius), axis=(0, 1))
    back_k = lagged[:KS, :KS]
    grad_scale = 1.0 / math.sqrt(TOKENS)
    return (grad_inputs, (sum_in * grad_scale).astype(jnp.bfloat16), (sum_out * grad_scale).astype(jnp.bfloat16), (back_k * grad_scale).astype(jnp.bfloat16))
```

```python
import math

import jax
import jax.numpy as jnp
from jax import lax
from jax.sharding import Mesh, PartitionSpec as P

KS = 27
ROW = ("yh", "x", "core")
COL = ("yl", "z")
PLANE = ("x", "yh", "yl")
LANES = 128


gelu_coef = 0.044715
root_coef = math.sqrt(2.0 / math.pi)


def padded_2(block, sides, width):
    for axis, dim in sides:
        count = lax.axis_size(axis)
        forward = [(i, i + 1) for i in range(count - 1)]
        backward = [(target, source) for source, target in forward]
        low = lax.ppermute(
            lax.slice_in_dim(block, block.shape[dim] - width, None, axis=dim), axis, forward
        )
        high = lax.ppermute(lax.slice_in_dim(block, 0, width, axis=dim), axis, backward)
        block = jnp.concatenate([low, block, high], axis=dim)
    return block


def gelu_parts(values):
    tanh_part = jnp.tanh(root_coef * (values + gelu_coef * values * values * values))
    result = 0.5 * values * (1.0 + tanh_part)
    slopes = 0.5 * (1.0 + tanh_part) + 0.5 * values * (1.0 - tanh_part * tanh_part) * root_coef * (
        1.0 + 3.0 * gelu_coef * values * values
    )
    return (result, slopes)


def to_rows(block):
    rows, cols = block.shape
    return block.reshape(rows // 8, 8, cols // LANES, LANES).transpose(0, 2, 1, 3).reshape(-1, LANES)


def from_rows(flat, shape):
    rows, cols = shape
    return flat.reshape(rows // 8, cols // LANES, 8, LANES).transpose(0, 2, 1, 3).reshape(rows, cols)


def scatter_sum(block, axes):
    count = lax.axis_size(axes)
    parts = block.reshape(count, block.shape[0] // count, LANES)
    arrived = lax.all_to_all(parts, axes, 0, 0)
    return jnp.sum(arrived.astype(jnp.float32), axis=0)


def gathered(block, axes):
    count = lax.axis_size(axes)
    copies = jnp.broadcast_to(block[None], (count,) + block.shape)
    return lax.all_to_all(copies, axes, 0, 0).reshape(count * block.shape[0], LANES)


def summed(blocks, scale):
    flat = jnp.concatenate([to_rows(block.astype(jnp.bfloat16)) for block in blocks], axis=0)
    half = scatter_sum(flat, "core")
    part = scatter_sum(half.astype(jnp.bfloat16), PLANE)
    total = (scatter_sum(part, "z") * scale).astype(jnp.bfloat16)
    return gathered(gathered(gathered(total, "z"), PLANE), "core")


def per_device(inputs, stored, upstream, weight_in, weight_out, kernel):
    tile_rows, tile_cols, channels = stored.shape
    radius = KS // 2
    padded_in = padded_2(inputs, ((ROW, 0), (COL, 1)), radius)
    flat_z = stored.reshape(tile_rows * tile_cols, channels)
    flat_g = upstream.reshape(tile_rows * tile_cols, channels)
    hidden = jnp.dot(flat_z, weight_in, preferred_element_type=jnp.float32)
    values, slopes = gelu_parts(hidden)
    active = values.astype(jnp.bfloat16)
    back_proj = jnp.einsum("nc,fc->nf", flat_g, weight_out, preferred_element_type=jnp.float32)
    grad_hidden = (back_proj * slopes).astype(jnp.bfloat16)
    grad_flat = (
        flat_g.astype(jnp.float32)
        + jnp.einsum("nf,cf->nc", grad_hidden, weight_in, preferred_element_type=jnp.float32)
    ).astype(jnp.bfloat16)
    sum_in = jnp.einsum("nc,nf->cf", flat_z, grad_hidden, preferred_element_type=jnp.float32)
    sum_out = jnp.einsum("nf,nc->fc", active, flat_g, preferred_element_type=jnp.float32)
    grad_mid = grad_flat.reshape(tile_rows, tile_cols, channels)
    padded = padded_2(grad_mid, ((ROW, 0), (COL, 1)), radius)
    kernel_wide = kernel.astype(jnp.float32)

    def sweep(row_off, state_pair):
        accumulated, kernel_sums = state_pair
        slab_rows = lax.dynamic_slice_in_dim(padded, 2 * radius - row_off, tile_rows, 0)
        tap_row = lax.dynamic_index_in_dim(kernel_wide, row_off, 0, keepdims=False)
        tap_sums = []
        source_rows = lax.dynamic_slice_in_dim(padded_in, row_off, tile_rows, 0)
        for offset in range(KS):
            shifted = slab_rows[:, 2 * radius - offset : 2 * radius - offset + tile_cols].astype(
                jnp.float32
            )
            accumulated = accumulated + tap_row[offset] * shifted
            tap_sums.append(
                jnp.sum(
                    source_rows[:, offset : offset + tile_cols].astype(jnp.float32)
                    * grad_mid.astype(jnp.float32),
                    axis=(0, 1),
                )
            )
        kernel_sums = lax.dynamic_update_index_in_dim(kernel_sums, jnp.stack(tap_sums), row_off, 0)
        return (accumulated, kernel_sums)

    start = (
        jnp.zeros((tile_rows, tile_cols, channels), jnp.float32),
        jnp.zeros((KS, KS, channels), jnp.float32),
    )
    accumulated, kernel_sums = lax.fori_loop(0, KS, sweep, start)
    grad_inputs = (grad_mid.astype(jnp.float32) + accumulated).astype(jnp.bfloat16)
    pixel_count = tile_rows * tile_cols * lax.axis_size(ROW) * lax.axis_size(COL)
    grad_scale = 1.0 / math.sqrt(pixel_count)
    taps = jnp.pad(kernel_sums.reshape(KS * KS, channels), ((0, 768 - KS * KS), (0, 0)))
    final = summed([sum_in, sum_out, taps], grad_scale)
    rows_in = sum_in.size // LANES
    final_in = from_rows(final[:rows_in], sum_in.shape)
    final_out = from_rows(final[rows_in : 2 * rows_in], sum_out.shape)
    final_kernel = from_rows(final[2 * rows_in :], taps.shape)[: KS * KS].reshape(KS, KS, channels)
    return (grad_inputs, final_in, final_out, final_kernel)


def solution(mesh):
    fine = Mesh(mesh.devices.reshape(2, 4, 2, 2, 16), ("yh", "x", "core", "yl", "z"))
    return jax.shard_map(
        per_device,
        mesh=fine,
        in_specs=(P(ROW, COL, None), P(ROW, COL, None), P(ROW, COL, None), P(), P(), P()),
        out_specs=(P(ROW, COL, None), P(), P(), P()),
        check_vma=False,
    )
```

```python
import functools
import math

import jax
import jax.numpy as jnp
import numpy as np
from jax import lax
from jax.experimental import pallas as pl
from jax.experimental.pallas import tpu as pltpu
from jax.sharding import Mesh, PartitionSpec as P

KS = 27
RADIUS = KS // 2
TILE = 16
PATCH = TILE + KS - 1
HALF = PATCH // 2 + 1
BAND = 24
CELLS = 2 * BAND // 8
ROW = ("yh", "x", "core")
COL = ("yl", "z")
PLANE = ("x", "yh", "yl")
LANES = 128


gelu_coef = 0.044715
root_coef = math.sqrt(2.0 / math.pi)


def split_stack(matrix, order):
    high = matrix.astype(jnp.bfloat16)
    low = (matrix - high.astype(np.float64)).astype(jnp.bfloat16)
    return np.concatenate([{"h": high, "l": low}[part] for part in order], axis=1)


def forward_matrix(positions):
    matrix = np.zeros((2 * BAND, len(positions)))
    freq = np.arange(HALF)
    for column, position in enumerate(positions):
        if position is not None:
            angle = 2.0 * np.pi * ((freq * position) % PATCH) / PATCH
            matrix[:HALF, column] = np.cos(angle)
            matrix[BAND : BAND + HALF, column] = -np.sin(angle)
    return split_stack(matrix, "hl")


def inverse_matrix(positions, rows):
    matrix = np.zeros((rows, 2 * BAND))
    freq = np.arange(HALF)
    weight = np.where((freq == 0) | (2 * freq == PATCH), 1.0, 2.0) / PATCH
    for row, position in enumerate(positions):
        angle = 2.0 * np.pi * ((freq * position) % PATCH) / PATCH
        matrix[row, :HALF] = weight * np.cos(angle)
        matrix[row, BAND : BAND + HALF] = -weight * np.sin(angle)
    return split_stack(matrix, "hlh")


PATCH_POSITIONS = [i - TILE + RADIUS if 0 <= i - TILE + RADIUS < PATCH else None for i in range(3 * TILE)]


def transform(matrix_ref, pieces, out_ref, count, unroll):
    def some(step, carry):
        for extra in range(unroll):
            row = step * unroll + extra
            pixels = jnp.concatenate([piece[row] for piece in pieces] * 2, axis=0)
            spectrum = jnp.dot(matrix_ref[...], pixels, preferred_element_type=jnp.float32)
            for lane in range(2):
                part = spectrum[:, lane * LANES : (lane + 1) * LANES]
                out_ref[row, lane * CELLS : (lane + 1) * CELLS] = part.reshape(CELLS, 8, LANES)
        return carry

    lax.fori_loop(0, count // unroll, some, 0)


def back(matrix_ref, spectrum_ref, row):
    lanes = [
        spectrum_ref[row, lane * CELLS : (lane + 1) * CELLS].reshape(2 * BAND, LANES) for lane in range(2)
    ]
    values = jnp.concatenate(lanes, axis=1)
    high = values.astype(jnp.bfloat16)
    low = (values - high.astype(jnp.float32)).astype(jnp.bfloat16)
    stacked = jnp.concatenate([high, high, low], axis=0)
    return jnp.dot(matrix_ref[...], stacked, preferred_element_type=jnp.float32)


def each_cell(work):
    def lane_step(lane, carry):
        def cell_step(cell, inner):
            work(lane * CELLS + cell, lane * CELLS + CELLS // 2 + cell)
            return inner

        return lax.fori_loop(0, CELLS // 2, cell_step, carry)

    lax.fori_loop(0, 2, lane_step, 0)


def taps_kernel(left, centre, right, grad, patch_mat, tile_mat, inv_mat, out_ref, wide, tile, sums):
    transform(patch_mat, [left, centre, right], wide, PATCH, 6)
    transform(tile_mat, [grad], tile, TILE, 4)
    block = 9

    def work(re, im):
        def block_step(index, carry):
            base = index * block
            real = [None] * block
            imag = [None] * block
            for i in range(TILE):
                gr, gi = tile[i, re], tile[i, im]
                for a in range(block):
                    xr, xi = wide[base + i + a, re], wide[base + i + a, im]
                    new_r = xr * gr + xi * gi
                    new_i = xi * gr - xr * gi
                    real[a] = new_r if i == 0 else real[a] + new_r
                    imag[a] = new_i if i == 0 else imag[a] + new_i
            for a in range(block):
                sums[base + a, re] = real[a]
                sums[base + a, im] = imag[a]
            return carry

        lax.fori_loop(0, KS // block, block_step, 0)

    each_cell(work)
    for a in range(KS):
        out_ref[a * KS : (a + 1) * KS, :] = back(inv_mat, sums, a)[:KS]
    out_ref[KS * KS :, :] = jnp.zeros((out_ref.shape[0] - KS * KS, out_ref.shape[1]), jnp.float32)


def conv_kernel(left, centre, right, taps, grad, patch_mat, taps_mat, inv_mat, out_ref, wide, filt, sums):
    transform(patch_mat, [left, centre, right], wide, PATCH, 6)
    transform(taps_mat, [taps], filt, KS, 3)
    block = 8

    def work(re, im):
        def block_step(index, carry):
            base = index * block
            real = [None] * block
            imag = [None] * block
            for a in range(KS):
                kr, ki = filt[a, re], filt[a, im]
                for i in range(block):
                    row = base + i + KS - 1 - a
                    gr, gi = wide[row, re], wide[row, im]
                    new_r = kr * gr - ki * gi
                    new_i = kr * gi + ki * gr
                    real[i] = new_r if a == 0 else real[i] + new_r
                    imag[i] = new_i if a == 0 else imag[i] + new_i
            for i in range(block):
                sums[base + i, re] = real[i]
                sums[base + i, im] = imag[i]
            return carry

        lax.fori_loop(0, TILE // block, block_step, 0)

    each_cell(work)
    for i in range(TILE):
        out_ref[i] = (grad[i].astype(jnp.float32) + back(inv_mat, sums, i)).astype(jnp.bfloat16)


def spectral_call(kernel, out_shape, second_rows, sum_rows, args):
    channels = args[0].shape[-1]
    return pl.pallas_call(
        kernel,
        out_shape=out_shape,
        in_specs=[pl.BlockSpec(memory_space=pltpu.VMEM)] * len(args),
        out_specs=pl.BlockSpec(memory_space=pltpu.VMEM),
        scratch_shapes=[
            pltpu.VMEM((PATCH, 2 * CELLS, 8, LANES), jnp.float32),
            pltpu.VMEM((second_rows, 2 * CELLS, 8, LANES), jnp.float32),
            pltpu.VMEM((sum_rows, 2 * CELLS, 8, LANES), jnp.float32),
        ],
        compiler_params=pltpu.CompilerParams(vmem_limit_bytes=32 << 20),
        cost_estimate=pl.CostEstimate(flops=4_000_000_000, bytes_accessed=8_000_000, transcendentals=0),
    )(*args)


def taps_gradient(sides, grad_tile):
    mats = (
        forward_matrix(PATCH_POSITIONS),
        forward_matrix(list(range(TILE))),
        inverse_matrix(range(KS), 32),
    )
    args = (*sides, grad_tile, *(jnp.asarray(m) for m in mats))
    out = jax.ShapeDtypeStruct((768, grad_tile.shape[-1]), jnp.float32)
    return spectral_call(taps_kernel, out, TILE, KS, args)


def conv_backward(sides, taps, grad_tile):
    mats = (
        forward_matrix(PATCH_POSITIONS),
        forward_matrix(list(range(KS)) + [None] * 5),
        inverse_matrix(range(KS - 1, PATCH), TILE),
    )
    padded = jnp.pad(taps, ((0, 0), (0, 32 - KS), (0, 0)))
    args = (*sides, padded, grad_tile, *(jnp.asarray(m) for m in mats))
    out = jax.ShapeDtypeStruct(grad_tile.shape, jnp.bfloat16)
    return spectral_call(conv_kernel, out, KS, TILE, args)


def shifted(block, axes, step):
    count = lax.axis_size(axes)
    pairs = [(i, i + step) for i in range(count) if 0 <= i + step < count]
    return lax.ppermute(block, axes, pairs)


def halo(block):
    low = shifted(block[-RADIUS:], ROW, 1)
    high = shifted(block[:RADIUS], ROW, -1)
    tall = jnp.concatenate([low, block, high], axis=0)
    return (shifted(tall, COL, 1), tall, shifted(tall, COL, -1))


def gelu_parts(values):
    tanh_part = jnp.tanh(root_coef * (values + gelu_coef * values * values * values))
    result = 0.5 * values * (1.0 + tanh_part)
    slopes = 0.5 * (1.0 + tanh_part) + 0.5 * values * (1.0 - tanh_part * tanh_part) * root_coef * (
        1.0 + 3.0 * gelu_coef * values * values
    )
    return (result, slopes)


def to_rows(block):
    rows, cols = block.shape
    return block.reshape(rows // 8, 8, cols // LANES, LANES).transpose(0, 2, 1, 3).reshape(-1, LANES)


def from_rows(flat, shape):
    rows, cols = shape
    return flat.reshape(rows // 8, cols // LANES, 8, LANES).transpose(0, 2, 1, 3).reshape(rows, cols)


def scatter_sum(block, axes):
    count = lax.axis_size(axes)
    parts = block.reshape(count, block.shape[0] // count, LANES)
    arrived = lax.all_to_all(parts, axes, 0, 0)
    return jnp.sum(arrived.astype(jnp.float32), axis=0)


def gathered(block, axes):
    count = lax.axis_size(axes)
    copies = jnp.broadcast_to(block[None], (count,) + block.shape)
    return lax.all_to_all(copies, axes, 0, 0).reshape(count * block.shape[0], LANES)


def summed(blocks, scale):
    flat = jnp.concatenate([to_rows(block.astype(jnp.bfloat16)) for block in blocks], axis=0)
    half = scatter_sum(flat, "core")
    part = scatter_sum(half.astype(jnp.bfloat16), PLANE)
    total = (scatter_sum(part, "z") * scale).astype(jnp.bfloat16)
    return gathered(gathered(gathered(total, "z"), PLANE), "core")


def per_device(inputs, stored, upstream, weight_in, weight_out, kernel):
    tile_rows, tile_cols, channels = stored.shape
    sides_in = halo(inputs)
    flat_z = stored.reshape(tile_rows * tile_cols, channels)
    flat_g = upstream.reshape(tile_rows * tile_cols, channels)
    hidden = jnp.dot(flat_z, weight_in, preferred_element_type=jnp.float32)
    values, slopes = gelu_parts(hidden)
    active = values.astype(jnp.bfloat16)
    back_proj = jnp.einsum("nc,fc->nf", flat_g, weight_out, preferred_element_type=jnp.float32)
    grad_hidden = (back_proj * slopes).astype(jnp.bfloat16)
    grad_flat = (
        flat_g.astype(jnp.float32)
        + jnp.einsum("nf,cf->nc", grad_hidden, weight_in, preferred_element_type=jnp.float32)
    ).astype(jnp.bfloat16)
    sum_in = jnp.einsum("nc,nf->cf", flat_z, grad_hidden, preferred_element_type=jnp.float32)
    sum_out = jnp.einsum("nf,nc->fc", active, flat_g, preferred_element_type=jnp.float32)
    grad_mid = grad_flat.reshape(tile_rows, tile_cols, channels)
    tap_sums = taps_gradient(sides_in, grad_mid)
    sides_mid = halo(grad_mid)
    grad_inputs = conv_backward(sides_mid, kernel, grad_mid)
    pixel_count = tile_rows * tile_cols * lax.axis_size(ROW) * lax.axis_size(COL)
    grad_scale = 1.0 / math.sqrt(pixel_count)
    final = summed([sum_in, sum_out, tap_sums], grad_scale)
    rows_in = sum_in.size // LANES
    final_in = from_rows(final[:rows_in], sum_in.shape)
    final_out = from_rows(final[rows_in : 2 * rows_in], sum_out.shape)
    final_kernel = from_rows(final[2 * rows_in :], tap_sums.shape)[: KS * KS].reshape(KS, KS, channels)
    return (grad_inputs, final_in, final_out, final_kernel)


def solution(mesh):
    fine = Mesh(mesh.devices.reshape(2, 4, 2, 2, 16), ("yh", "x", "core", "yl", "z"))
    return jax.shard_map(
        per_device,
        mesh=fine,
        in_specs=(P(ROW, COL, None), P(ROW, COL, None), P(ROW, COL, None), P(), P(), P()),
        out_specs=(P(ROW, COL, None), P(), P(), P()),
        check_vma=False,
    )
```

```python
import math

import jax
import jax.numpy as jnp
import numpy as np
from jax import lax
from jax.experimental import pallas as pl
from jax.experimental.pallas import tpu as pltpu
from jax.sharding import Mesh, PartitionSpec as P

KS = 27
RADIUS = KS // 2
TILE = 16
PATCH = TILE + KS - 1
HALF = PATCH // 2 + 1
BAND = 24
CELLS = 2 * BAND // 8
ROW = ("yh", "x", "core")
COL = ("yl", "z")
PLANE = ("x", "yh", "yl")
LANES = 128


gelu_coef = 0.044715
root_coef = math.sqrt(2.0 / math.pi)


def split_stack(matrix, order):
    high = matrix.astype(jnp.bfloat16)
    low = (matrix - high.astype(np.float64)).astype(jnp.bfloat16)
    return np.concatenate([{"h": high, "l": low}[part] for part in order], axis=1)


def forward_matrix(positions):
    matrix = np.zeros((2 * BAND, len(positions)))
    freq = np.arange(HALF)
    for column, position in enumerate(positions):
        if position is not None:
            angle = 2.0 * np.pi * ((freq * position) % PATCH) / PATCH
            matrix[:HALF, column] = np.cos(angle)
            matrix[BAND : BAND + HALF, column] = -np.sin(angle)
    return split_stack(matrix, "hl")


def inverse_matrix(positions, rows):
    matrix = np.zeros((rows, 2 * BAND))
    freq = np.arange(HALF)
    weight = np.where((freq == 0) | (2 * freq == PATCH), 1.0, 2.0) / PATCH
    for row, position in enumerate(positions):
        angle = 2.0 * np.pi * ((freq * position) % PATCH) / PATCH
        matrix[row, :HALF] = weight * np.cos(angle)
        matrix[row, BAND : BAND + HALF] = -weight * np.sin(angle)
    return split_stack(matrix, "hlh")


PATCH_POSITIONS = [i - TILE + RADIUS if 0 <= i - TILE + RADIUS < PATCH else None for i in range(3 * TILE)]


def transform(matrix_ref, pixels_ref, out_ref, first, unroll):
    def some(step, carry):
        for extra in range(unroll):
            row = step * unroll + extra
            pixels = jnp.concatenate([pixels_ref[row]] * 2, axis=0)
            spectrum = jnp.dot(matrix_ref[...], pixels, preferred_element_type=jnp.float32)
            for lane in range(2):
                part = spectrum[:, lane * LANES : (lane + 1) * LANES]
                out_ref[first + row, lane * CELLS : (lane + 1) * CELLS] = part.reshape(CELLS, 8, LANES)
        return carry

    lax.fori_loop(0, pixels_ref.shape[0] // unroll, some, 0)


def transform_patch(matrix_ref, low, wide, high, out_ref):
    transform(matrix_ref, low, out_ref, 0, low.shape[0])
    transform(matrix_ref, wide, out_ref, RADIUS, 8)
    transform(matrix_ref, high, out_ref, RADIUS + TILE, high.shape[0])


def back(matrix_ref, spectrum_ref, row):
    lanes = [
        spectrum_ref[row, lane * CELLS : (lane + 1) * CELLS].reshape(2 * BAND, LANES) for lane in range(2)
    ]
    values = jnp.concatenate(lanes, axis=1)
    high = values.astype(jnp.bfloat16)
    low = (values - high.astype(jnp.float32)).astype(jnp.bfloat16)
    stacked = jnp.concatenate([high, high, low], axis=0)
    return jnp.dot(matrix_ref[...], stacked, preferred_element_type=jnp.float32)


def each_cell(work):
    def lane_step(lane, carry):
        def cell_step(cell, inner):
            work(lane * CELLS + cell, lane * CELLS + CELLS // 2 + cell)
            return inner

        return lax.fori_loop(0, CELLS // 2, cell_step, carry)

    lax.fori_loop(0, 2, lane_step, 0)


def taps_kernel(low, centre, high, grad, patch_mat, tile_mat, inv_mat, out_ref, wide, tile, sums):
    transform(tile_mat, grad, tile, 0, 8)
    transform_patch(patch_mat, low, centre, high, wide)
    block = 9

    def work(re, im):
        def block_step(index, carry):
            base = index * block
            real = [None] * block
            imag = [None] * block
            for i in range(TILE):
                gr, gi = tile[i, re], tile[i, im]
                for a in range(block):
                    xr, xi = wide[base + i + a, re], wide[base + i + a, im]
                    new_r = xr * gr + xi * gi
                    new_i = xi * gr - xr * gi
                    real[a] = new_r if i == 0 else real[a] + new_r
                    imag[a] = new_i if i == 0 else imag[a] + new_i
            for a in range(block):
                sums[base + a, re] = real[a]
                sums[base + a, im] = imag[a]
            return carry

        lax.fori_loop(0, KS // block, block_step, 0)

    each_cell(work)
    for a in range(KS):
        out_ref[a * KS : (a + 1) * KS, :] = back(inv_mat, sums, a)[:KS]
    out_ref[KS * KS :, :] = jnp.zeros((out_ref.shape[0] - KS * KS, out_ref.shape[1]), jnp.float32)


def conv_kernel(low, centre, high, taps, grad, patch_mat, taps_mat, inv_mat, out_ref, wide, filt, sums):
    transform(taps_mat, taps, filt, 0, 9)
    transform_patch(patch_mat, low, centre, high, wide)
    block = 8

    def work(re, im):
        def block_step(index, carry):
            base = index * block
            real = [None] * block
            imag = [None] * block
            for a in range(KS):
                kr, ki = filt[a, re], filt[a, im]
                for i in range(block):
                    row = base + i + KS - 1 - a
                    gr, gi = wide[row, re], wide[row, im]
                    new_r = kr * gr - ki * gi
                    new_i = kr * gi + ki * gr
                    real[i] = new_r if a == 0 else real[i] + new_r
                    imag[i] = new_i if a == 0 else imag[i] + new_i
            for i in range(block):
                sums[base + i, re] = real[i]
                sums[base + i, im] = imag[i]
            return carry

        lax.fori_loop(0, TILE // block, block_step, 0)

    each_cell(work)
    for i in range(TILE):
        out_ref[i] = (grad[i].astype(jnp.float32) + back(inv_mat, sums, i)).astype(jnp.bfloat16)


def spectral_call(kernel, out_shape, second_rows, sum_rows, args):
    channels = args[0].shape[-1]
    return pl.pallas_call(
        kernel,
        out_shape=out_shape,
        in_specs=[pl.BlockSpec(memory_space=pltpu.VMEM)] * len(args),
        out_specs=pl.BlockSpec(memory_space=pltpu.VMEM),
        scratch_shapes=[
            pltpu.VMEM((PATCH, 2 * CELLS, 8, LANES), jnp.float32),
            pltpu.VMEM((second_rows, 2 * CELLS, 8, LANES), jnp.float32),
            pltpu.VMEM((sum_rows, 2 * CELLS, 8, LANES), jnp.float32),
        ],
        compiler_params=pltpu.CompilerParams(vmem_limit_bytes=32 << 20),
        cost_estimate=pl.CostEstimate(flops=4_000_000_000, bytes_accessed=8_000_000, transcendentals=0),
    )(*args)


def taps_gradient(sides, grad_tile):
    mats = (
        forward_matrix(PATCH_POSITIONS),
        forward_matrix(list(range(TILE))),
        inverse_matrix(range(KS), 32),
    )
    args = (*sides, grad_tile, *(jnp.asarray(m) for m in mats))
    out = jax.ShapeDtypeStruct((768, grad_tile.shape[-1]), jnp.float32)
    return spectral_call(taps_kernel, out, TILE, KS, args)


def conv_backward(sides, taps, grad_tile):
    mats = (
        forward_matrix(PATCH_POSITIONS),
        forward_matrix(list(range(KS)) + [None] * 5),
        inverse_matrix(range(KS - 1, PATCH), TILE),
    )
    padded = jnp.pad(taps, ((0, 0), (0, 32 - KS), (0, 0)))
    args = (*sides, padded, grad_tile, *(jnp.asarray(m) for m in mats))
    out = jax.ShapeDtypeStruct(grad_tile.shape, jnp.bfloat16)
    return spectral_call(conv_kernel, out, KS, TILE, args)


def shifted(block, axes, step):
    count = lax.axis_size(axes)
    pairs = [(i, i + step) for i in range(count) if 0 <= i + step < count]
    return lax.ppermute(block, axes, pairs)


def halo(block):
    wide = jnp.concatenate([shifted(block, COL, 1), block, shifted(block, COL, -1)], axis=1)
    low = shifted(wide[-RADIUS:], ROW, 1)
    high = shifted(wide[:RADIUS], ROW, -1)
    return (low, wide, high)


def gelu_parts(values):
    tanh_part = jnp.tanh(root_coef * (values + gelu_coef * values * values * values))
    result = 0.5 * values * (1.0 + tanh_part)
    slopes = 0.5 * (1.0 + tanh_part) + 0.5 * values * (1.0 - tanh_part * tanh_part) * root_coef * (
        1.0 + 3.0 * gelu_coef * values * values
    )
    return (result, slopes)


def to_rows(block):
    rows, cols = block.shape
    return block.reshape(rows // 8, 8, cols // LANES, LANES).transpose(0, 2, 1, 3).reshape(-1, LANES)


def from_rows(flat, shape):
    rows, cols = shape
    return flat.reshape(rows // 8, cols // LANES, 8, LANES).transpose(0, 2, 1, 3).reshape(rows, cols)


def scatter_sum(block, axes):
    count = lax.axis_size(axes)
    parts = block.reshape(count, block.shape[0] // count, LANES)
    arrived = lax.all_to_all(parts, axes, 0, 0)
    return jnp.sum(arrived.astype(jnp.float32), axis=0)


def gathered(block, axes):
    count = lax.axis_size(axes)
    copies = jnp.broadcast_to(block[None], (count,) + block.shape)
    return lax.all_to_all(copies, axes, 0, 0).reshape(count * block.shape[0], LANES)


def summed(dense, taps, scale):
    halves = []
    for blocks in (dense, [taps]):
        flat = jnp.concatenate([to_rows(block.astype(jnp.bfloat16)) for block in blocks], axis=0)
        halves.append(scatter_sum(flat, "core").astype(jnp.bfloat16))
    part = scatter_sum(jnp.concatenate(halves, axis=0), PLANE)
    total = (scatter_sum(part, "z") * scale).astype(jnp.bfloat16)
    both = gathered(gathered(gathered(total, "z"), PLANE), "core").reshape(2, -1, LANES)
    split = halves[0].shape[0]
    return both[:, :split].reshape(-1, LANES), both[:, split:].reshape(-1, LANES)


def per_device(inputs, stored, upstream, weight_in, weight_out, kernel):
    tile_rows, tile_cols, channels = stored.shape
    sides_in = halo(inputs)
    flat_z = stored.reshape(tile_rows * tile_cols, channels)
    flat_g = upstream.reshape(tile_rows * tile_cols, channels)
    hidden = jnp.dot(flat_z, weight_in, preferred_element_type=jnp.float32)
    values, slopes = gelu_parts(hidden)
    active = values.astype(jnp.bfloat16)
    back_proj = jnp.einsum("nc,fc->nf", flat_g, weight_out, preferred_element_type=jnp.float32)
    grad_hidden = (back_proj * slopes).astype(jnp.bfloat16)
    grad_flat = (
        flat_g.astype(jnp.float32)
        + jnp.einsum("nf,cf->nc", grad_hidden, weight_in, preferred_element_type=jnp.float32)
    ).astype(jnp.bfloat16)
    sum_in = jnp.einsum("nc,nf->cf", flat_z, grad_hidden, preferred_element_type=jnp.float32)
    sum_out = jnp.einsum("nf,nc->fc", active, flat_g, preferred_element_type=jnp.float32)
    grad_mid = grad_flat.reshape(tile_rows, tile_cols, channels)
    tap_sums = taps_gradient(sides_in, grad_mid)
    sides_mid = halo(grad_mid)
    grad_inputs = conv_backward(sides_mid, kernel, grad_mid)
    pixel_count = tile_rows * tile_cols * lax.axis_size(ROW) * lax.axis_size(COL)
    grad_scale = 1.0 / math.sqrt(pixel_count)
    final_dense, final_taps = summed([sum_in, sum_out], tap_sums, grad_scale)
    rows_in = sum_in.size // LANES
    final_in = from_rows(final_dense[:rows_in], sum_in.shape)
    final_out = from_rows(final_dense[rows_in:], sum_out.shape)
    final_kernel = from_rows(final_taps, tap_sums.shape)[: KS * KS].reshape(KS, KS, channels)
    return (grad_inputs, final_in, final_out, final_kernel)


def solution(mesh):
    fine = Mesh(mesh.devices.reshape(2, 4, 2, 2, 16), ("yh", "x", "core", "yl", "z"))
    return jax.shard_map(
        per_device,
        mesh=fine,
        in_specs=(P(ROW, COL, None), P(ROW, COL, None), P(ROW, COL, None), P(), P(), P()),
        out_specs=(P(ROW, COL, None), P(), P(), P()),
        check_vma=False,
    )
```

```python
import math

import jax
import jax.numpy as jnp
import numpy as np
from jax import lax
from jax.experimental import pallas as pl
from jax.experimental.pallas import tpu as pltpu
from jax.sharding import Mesh, PartitionSpec as P

KS = 27
RADIUS = KS // 2
TILE = 16
PATCH = TILE + KS - 1
HALF = PATCH // 2 + 1
BAND = 24
CELLS = 2 * BAND // 8
ROW = ("yh", "x", "core")
COL = ("yl", "z")
PLANE = ("x", "yh", "yl")
LANES = 128


gelu_coef = 0.044715
root_coef = math.sqrt(2.0 / math.pi)


def split_stack(matrix, order):
    high = matrix.astype(jnp.bfloat16)
    low = (matrix - high.astype(np.float64)).astype(jnp.bfloat16)
    return np.concatenate([{"h": high, "l": low}[part] for part in order], axis=1)


def forward_matrix(positions):
    matrix = np.zeros((2 * BAND, len(positions)))
    freq = np.arange(HALF)
    for column, position in enumerate(positions):
        if position is not None:
            angle = 2.0 * np.pi * ((freq * position) % PATCH) / PATCH
            matrix[:HALF, column] = np.cos(angle)
            matrix[BAND : BAND + HALF, column] = -np.sin(angle)
    return split_stack(matrix, "hl")


def inverse_matrix(positions, rows):
    matrix = np.zeros((rows, 2 * BAND))
    freq = np.arange(HALF)
    weight = np.where((freq == 0) | (2 * freq == PATCH), 1.0, 2.0) / PATCH
    for row, position in enumerate(positions):
        angle = 2.0 * np.pi * ((freq * position) % PATCH) / PATCH
        matrix[row, :HALF] = weight * np.cos(angle)
        matrix[row, BAND : BAND + HALF] = -weight * np.sin(angle)
    return split_stack(matrix, "hlh")


PATCH_POSITIONS = [i - TILE + RADIUS if 0 <= i - TILE + RADIUS < PATCH else None for i in range(3 * TILE)]


def transform(matrix_ref, pixels_ref, out_ref, first, unroll):
    def some(step, carry):
        for extra in range(unroll):
            row = step * unroll + extra
            pixels = jnp.concatenate([pixels_ref[row]] * 2, axis=0)
            spectrum = jnp.dot(matrix_ref[...], pixels, preferred_element_type=jnp.float32)
            for lane in range(2):
                part = spectrum[:, lane * LANES : (lane + 1) * LANES]
                out_ref[first + row, lane * CELLS : (lane + 1) * CELLS] = part.reshape(CELLS, 8, LANES)
        return carry

    lax.fori_loop(0, pixels_ref.shape[0] // unroll, some, 0)


def transform_patch(matrix_ref, low, wide, high, out_ref):
    transform(matrix_ref, low, out_ref, 0, low.shape[0])
    transform(matrix_ref, wide, out_ref, RADIUS, 8)
    transform(matrix_ref, high, out_ref, RADIUS + TILE, high.shape[0])


def back(matrix_ref, spectrum_ref, row):
    lanes = [
        spectrum_ref[row, lane * CELLS : (lane + 1) * CELLS].reshape(2 * BAND, LANES) for lane in range(2)
    ]
    values = jnp.concatenate(lanes, axis=1)
    high = values.astype(jnp.bfloat16)
    low = (values - high.astype(jnp.float32)).astype(jnp.bfloat16)
    stacked = jnp.concatenate([high, high, low], axis=0)
    return jnp.dot(matrix_ref[...], stacked, preferred_element_type=jnp.float32)


def each_cell(work):
    def lane_step(lane, carry):
        def cell_step(cell, inner):
            work(lane * CELLS + cell, lane * CELLS + CELLS // 2 + cell)
            return inner

        return lax.fori_loop(0, CELLS // 2, cell_step, carry)

    lax.fori_loop(0, 2, lane_step, 0)


def taps_kernel(low, centre, high, own, patch_mat, tile_mat, inv_mat, out_ref, wide, tile, sums):
    transform(tile_mat, own, tile, 0, 8)
    transform_patch(patch_mat, low, centre, high, wide)
    block = 9

    def work(re, im):
        def block_step(index, carry):
            base = index * block
            real = [None] * block
            imag = [None] * block
            for i in range(TILE):
                xr, xi = tile[i, re], tile[i, im]
                for a in range(block):
                    row = i + KS - 1 - base - a
                    gr, gi = wide[row, re], wide[row, im]
                    new_r = xr * gr + xi * gi
                    new_i = xr * gi - xi * gr
                    real[a] = new_r if i == 0 else real[a] + new_r
                    imag[a] = new_i if i == 0 else imag[a] + new_i
            for a in range(block):
                sums[base + a, re] = real[a]
                sums[base + a, im] = imag[a]
            return carry

        lax.fori_loop(0, KS // block, block_step, 0)

    each_cell(work)
    for a in range(KS):
        out_ref[a * KS : (a + 1) * KS, :] = back(inv_mat, sums, a)[:KS]
    out_ref[KS * KS :, :] = jnp.zeros((out_ref.shape[0] - KS * KS, out_ref.shape[1]), jnp.float32)


def conv_kernel(low, centre, high, taps, grad, patch_mat, taps_mat, inv_mat, out_ref, wide, filt, sums):
    transform(taps_mat, taps, filt, 0, 9)
    transform_patch(patch_mat, low, centre, high, wide)
    block = 8

    def work(re, im):
        def block_step(index, carry):
            base = index * block
            real = [None] * block
            imag = [None] * block
            for a in range(KS):
                kr, ki = filt[a, re], filt[a, im]
                for i in range(block):
                    row = base + i + KS - 1 - a
                    gr, gi = wide[row, re], wide[row, im]
                    new_r = kr * gr - ki * gi
                    new_i = kr * gi + ki * gr
                    real[i] = new_r if a == 0 else real[i] + new_r
                    imag[i] = new_i if a == 0 else imag[i] + new_i
            for i in range(block):
                sums[base + i, re] = real[i]
                sums[base + i, im] = imag[i]
            return carry

        lax.fori_loop(0, TILE // block, block_step, 0)

    each_cell(work)
    for i in range(TILE):
        out_ref[i] = (grad[i].astype(jnp.float32) + back(inv_mat, sums, i)).astype(jnp.bfloat16)


def spectral_call(kernel, out_shape, second_rows, sum_rows, args):
    channels = args[0].shape[-1]
    return pl.pallas_call(
        kernel,
        out_shape=out_shape,
        in_specs=[pl.BlockSpec(memory_space=pltpu.VMEM)] * len(args),
        out_specs=pl.BlockSpec(memory_space=pltpu.VMEM),
        scratch_shapes=[
            pltpu.VMEM((PATCH, 2 * CELLS, 8, LANES), jnp.float32),
            pltpu.VMEM((second_rows, 2 * CELLS, 8, LANES), jnp.float32),
            pltpu.VMEM((sum_rows, 2 * CELLS, 8, LANES), jnp.float32),
        ],
        compiler_params=pltpu.CompilerParams(vmem_limit_bytes=32 << 20),
        cost_estimate=pl.CostEstimate(flops=4_000_000_000, bytes_accessed=8_000_000, transcendentals=0),
    )(*args)


def taps_gradient(sides, own):
    mats = (
        forward_matrix(PATCH_POSITIONS),
        forward_matrix(list(range(TILE))),
        inverse_matrix(range(KS - 1, -1, -1), 32),
    )
    args = (*sides, own, *(jnp.asarray(m) for m in mats))
    out = jax.ShapeDtypeStruct((768, own.shape[-1]), jnp.float32)
    return spectral_call(taps_kernel, out, TILE, KS, args)


def conv_backward(sides, taps, grad_tile):
    mats = (
        forward_matrix(PATCH_POSITIONS),
        forward_matrix(list(range(KS)) + [None] * 5),
        inverse_matrix(range(KS - 1, PATCH), TILE),
    )
    padded = jnp.pad(taps, ((0, 0), (0, 32 - KS), (0, 0)))
    args = (*sides, padded, grad_tile, *(jnp.asarray(m) for m in mats))
    out = jax.ShapeDtypeStruct(grad_tile.shape, jnp.bfloat16)
    return spectral_call(conv_kernel, out, KS, TILE, args)


def shifted(block, axes, step):
    count = lax.axis_size(axes)
    pairs = [(i, i + step) for i in range(count) if 0 <= i + step < count]
    return lax.ppermute(block, axes, pairs)


def column_sides(block):
    runs, depth = lax.axis_size("yl"), lax.axis_size("z")
    ends = [(run * depth + depth - 1, (run + 1) * depth + depth - 1) for run in range(runs - 1)]
    ends += [((run + 1) * depth, run * depth) for run in range(runs - 1)]
    seam = lax.ppermute(block, COL, ends)
    place = lax.axis_index("z")
    up = jnp.where(place == depth - 1, seam, block)
    down = jnp.where(place == 0, seam, block)
    left = lax.ppermute(up, "z", [(i, (i + 1) % depth) for i in range(depth)])
    right = lax.ppermute(down, "z", [(i, (i - 1) % depth) for i in range(depth)])
    return left, right


def halo(block):
    left, right = column_sides(block)
    wide = jnp.concatenate([left, block, right], axis=1)
    low = shifted(wide[-RADIUS:], ROW, 1)
    high = shifted(wide[:RADIUS], ROW, -1)
    return (low, wide, high)


def gelu_parts(values):
    tanh_part = jnp.tanh(root_coef * (values + gelu_coef * values * values * values))
    result = 0.5 * values * (1.0 + tanh_part)
    slopes = 0.5 * (1.0 + tanh_part) + 0.5 * values * (1.0 - tanh_part * tanh_part) * root_coef * (
        1.0 + 3.0 * gelu_coef * values * values
    )
    return (result, slopes)


def to_rows(block):
    rows, cols = block.shape
    return block.reshape(rows // 8, 8, cols // LANES, LANES).transpose(0, 2, 1, 3).reshape(-1, LANES)


def from_rows(flat, shape):
    rows, cols = shape
    return flat.reshape(rows // 8, cols // LANES, 8, LANES).transpose(0, 2, 1, 3).reshape(rows, cols)


def scatter_sum(block, axes):
    count = lax.axis_size(axes)
    parts = block.reshape(count, block.shape[0] // count, LANES)
    arrived = lax.all_to_all(parts, axes, 0, 0)
    return jnp.sum(arrived.astype(jnp.float32), axis=0)


def gathered(block, axes):
    count = lax.axis_size(axes)
    copies = jnp.broadcast_to(block[None], (count,) + block.shape)
    return lax.all_to_all(copies, axes, 0, 0).reshape(count * block.shape[0], LANES)


def summed(dense, taps, scale):
    halves = []
    for blocks in (dense, [taps]):
        flat = jnp.concatenate([to_rows(block.astype(jnp.bfloat16)) for block in blocks], axis=0)
        halves.append(scatter_sum(flat, "core").astype(jnp.bfloat16))
    part = scatter_sum(jnp.concatenate(halves, axis=0), PLANE)
    total = (scatter_sum(part, "z") * scale).astype(jnp.bfloat16)
    both = gathered(gathered(gathered(total, "z"), PLANE), "core").reshape(2, -1, LANES)
    split = halves[0].shape[0]
    return both[:, :split].reshape(-1, LANES), both[:, split:].reshape(-1, LANES)


def per_device(inputs, stored, upstream, weight_in, weight_out, kernel):
    tile_rows, tile_cols, channels = stored.shape
    flat_z = stored.reshape(tile_rows * tile_cols, channels)
    flat_g = upstream.reshape(tile_rows * tile_cols, channels)
    hidden = jnp.dot(flat_z, weight_in, preferred_element_type=jnp.float32)
    values, slopes = gelu_parts(hidden)
    active = values.astype(jnp.bfloat16)
    back_proj = jnp.einsum("nc,fc->nf", flat_g, weight_out, preferred_element_type=jnp.float32)
    grad_hidden = (back_proj * slopes).astype(jnp.bfloat16)
    grad_flat = (
        flat_g.astype(jnp.float32)
        + jnp.einsum("nf,cf->nc", grad_hidden, weight_in, preferred_element_type=jnp.float32)
    ).astype(jnp.bfloat16)
    sum_in = jnp.einsum("nc,nf->cf", flat_z, grad_hidden, preferred_element_type=jnp.float32)
    sum_out = jnp.einsum("nf,nc->fc", active, flat_g, preferred_element_type=jnp.float32)
    grad_mid = grad_flat.reshape(tile_rows, tile_cols, channels)
    sides_mid = halo(grad_mid)
    tap_sums = taps_gradient(sides_mid, inputs)
    grad_inputs = conv_backward(sides_mid, kernel, grad_mid)
    pixel_count = tile_rows * tile_cols * lax.axis_size(ROW) * lax.axis_size(COL)
    grad_scale = 1.0 / math.sqrt(pixel_count)
    final_dense, final_taps = summed([sum_in, sum_out], tap_sums, grad_scale)
    rows_in = sum_in.size // LANES
    final_in = from_rows(final_dense[:rows_in], sum_in.shape)
    final_out = from_rows(final_dense[rows_in:], sum_out.shape)
    final_kernel = from_rows(final_taps, tap_sums.shape)[: KS * KS].reshape(KS, KS, channels)
    return (grad_inputs, final_in, final_out, final_kernel)


def solution(mesh):
    fine = Mesh(mesh.devices.reshape(2, 4, 2, 2, 16), ("yh", "x", "core", "yl", "z"))
    return jax.shard_map(
        per_device,
        mesh=fine,
        in_specs=(P(ROW, COL, None), P(ROW, COL, None), P(ROW, COL, None), P(), P(), P()),
        out_specs=(P(ROW, COL, None), P(), P(), P()),
        check_vma=False,
    )
```

```python
import math

import jax
import jax.numpy as jnp
import numpy as np
from jax import lax
from jax.experimental import pallas as pl
from jax.experimental.pallas import tpu as pltpu
from jax.sharding import Mesh, PartitionSpec as P


KS = 27
RADIUS = KS // 2
TILE = 16
PATCH = TILE + KS - 1
HALF = PATCH // 2 + 1
BAND = 24
CELLS = 2 * BAND // 8
ROW = ("yh", "x", "core")
COL = ("yl", "z")
PLANE = ("x", "yh", "yl")
LANES = 128


gelu_coef = 0.044715
root_coef = math.sqrt(2.0 / math.pi)


def split_stack(matrix, order):
    high = matrix.astype(jnp.bfloat16)
    low = (matrix - high.astype(np.float64)).astype(jnp.bfloat16)
    return np.concatenate([{"h": high, "l": low}[part] for part in order], axis=1)


def forward_matrix(positions):
    matrix = np.zeros((2 * BAND, len(positions)))
    freq = np.arange(HALF)
    for column, position in enumerate(positions):
        if position is not None:
            angle = 2.0 * np.pi * ((freq * position) % PATCH) / PATCH
            matrix[:HALF, column] = np.cos(angle)
            matrix[BAND : BAND + HALF, column] = -np.sin(angle)
    return split_stack(matrix, "hl")


def inverse_matrix(positions, rows):
    matrix = np.zeros((rows, 2 * BAND))
    freq = np.arange(HALF)
    weight = np.where((freq == 0) | (2 * freq == PATCH), 1.0, 2.0) / PATCH
    for row, position in enumerate(positions):
        angle = 2.0 * np.pi * ((freq * position) % PATCH) / PATCH
        matrix[row, :HALF] = weight * np.cos(angle)
        matrix[row, BAND : BAND + HALF] = -weight * np.sin(angle)
    return split_stack(matrix, "hlh")


PATCH_POSITIONS = [i - TILE + RADIUS if 0 <= i - TILE + RADIUS < PATCH else None for i in range(3 * TILE)]


def transform(matrix_ref, pixels_ref, out_ref, first, unroll):
    def some(step, carry):
        for extra in range(unroll):
            row = step * unroll + extra
            pixels = jnp.concatenate([pixels_ref[row]] * 2, axis=0)
            spectrum = jnp.dot(matrix_ref[...], pixels, preferred_element_type=jnp.float32)
            for lane in range(2):
                part = spectrum[:, lane * LANES : (lane + 1) * LANES]
                out_ref[first + row, lane * CELLS : (lane + 1) * CELLS] = part.reshape(CELLS, 8, LANES)
        return carry

    lax.fori_loop(0, pixels_ref.shape[0] // unroll, some, 0)


def transform_patch(matrix_ref, low, wide, high, out_ref):
    transform(matrix_ref, low, out_ref, 0, low.shape[0])
    transform(matrix_ref, wide, out_ref, RADIUS, 8)
    transform(matrix_ref, high, out_ref, RADIUS + TILE, high.shape[0])


def back(matrix_ref, spectrum_ref, row):
    lanes = [
        spectrum_ref[row, lane * CELLS : (lane + 1) * CELLS].reshape(2 * BAND, LANES) for lane in range(2)
    ]
    values = jnp.concatenate(lanes, axis=1)
    high = values.astype(jnp.bfloat16)
    low = (values - high.astype(jnp.float32)).astype(jnp.bfloat16)
    stacked = jnp.concatenate([high, high, low], axis=0)
    return jnp.dot(matrix_ref[...], stacked, preferred_element_type=jnp.float32)


def each_cell(work):
    def lane_step(lane, carry):
        def cell_step(cell, inner):
            work(lane * CELLS + cell, lane * CELLS + CELLS // 2 + cell)
            return inner

        return lax.fori_loop(0, CELLS // 2, cell_step, carry)

    lax.fori_loop(0, 2, lane_step, 0)


def taps_kernel(low, centre, high, own, patch_mat, tile_mat, inv_mat, out_ref, wide, tile, sums):
    transform(tile_mat, own, tile, 0, 8)
    transform_patch(patch_mat, low, centre, high, wide)
    block = 9

    def work(re, im):
        def block_step(index, carry):
            base = index * block
            real = [None] * block
            imag = [None] * block
            for i in range(TILE):
                xr, xi = tile[i, re], tile[i, im]
                for a in range(block):
                    row = i + KS - 1 - base - a
                    gr, gi = wide[row, re], wide[row, im]
                    new_r = xr * gr + xi * gi
                    new_i = xr * gi - xi * gr
                    real[a] = new_r if i == 0 else real[a] + new_r
                    imag[a] = new_i if i == 0 else imag[a] + new_i
            for a in range(block):
                sums[base + a, re] = real[a]
                sums[base + a, im] = imag[a]
            return carry

        lax.fori_loop(0, KS // block, block_step, 0)

    each_cell(work)
    for a in range(KS):
        out_ref[a * KS : (a + 1) * KS, :] = back(inv_mat, sums, a)[:KS]
    out_ref[KS * KS :, :] = jnp.zeros((out_ref.shape[0] - KS * KS, out_ref.shape[1]), jnp.float32)


def conv_kernel(low, centre, high, taps, grad, patch_mat, taps_mat, inv_mat, out_ref, wide, filt, sums):
    transform(taps_mat, taps, filt, 0, 9)
    transform_patch(patch_mat, low, centre, high, wide)
    block = 8

    def work(re, im):
        def block_step(index, carry):
            base = index * block
            real = [None] * block
            imag = [None] * block
            for a in range(KS):
                kr, ki = filt[a, re], filt[a, im]
                for i in range(block):
                    row = base + i + KS - 1 - a
                    gr, gi = wide[row, re], wide[row, im]
                    new_r = kr * gr - ki * gi
                    new_i = kr * gi + ki * gr
                    real[i] = new_r if a == 0 else real[i] + new_r
                    imag[i] = new_i if a == 0 else imag[i] + new_i
            for i in range(block):
                sums[base + i, re] = real[i]
                sums[base + i, im] = imag[i]
            return carry

        lax.fori_loop(0, TILE // block, block_step, 0)

    each_cell(work)
    for i in range(TILE):
        out_ref[i] = (grad[i].astype(jnp.float32) + back(inv_mat, sums, i)).astype(jnp.bfloat16)


def spectral_call(kernel, out_shape, second_rows, sum_rows, args):
    return pl.pallas_call(
        kernel,
        out_shape=out_shape,
        in_specs=[pl.BlockSpec(memory_space=pltpu.VMEM)] * len(args),
        out_specs=pl.BlockSpec(memory_space=pltpu.VMEM),
        scratch_shapes=[
            pltpu.VMEM((PATCH, 2 * CELLS, 8, LANES), jnp.float32),
            pltpu.VMEM((second_rows, 2 * CELLS, 8, LANES), jnp.float32),
            pltpu.VMEM((sum_rows, 2 * CELLS, 8, LANES), jnp.float32),
        ],
        compiler_params=pltpu.CompilerParams(vmem_limit_bytes=32 << 20),
        cost_estimate=pl.CostEstimate(flops=4_000_000_000, bytes_accessed=8_000_000, transcendentals=0),
    )(*args)


def taps_gradient(sides, own):
    mats = (
        forward_matrix(PATCH_POSITIONS),
        forward_matrix(list(range(TILE))),
        inverse_matrix(range(KS - 1, -1, -1), 32),
    )
    args = (*sides, own, *(jnp.asarray(m) for m in mats))
    out = jax.ShapeDtypeStruct((768, own.shape[-1]), jnp.float32)
    return spectral_call(taps_kernel, out, TILE, KS, args)


def conv_backward(sides, taps, grad_tile):
    mats = (
        forward_matrix(PATCH_POSITIONS),
        forward_matrix(list(range(KS)) + [None] * 5),
        inverse_matrix(range(KS - 1, PATCH), TILE),
    )
    padded = jnp.pad(taps, ((0, 0), (0, 32 - KS), (0, 0)))
    args = (*sides, padded, grad_tile, *(jnp.asarray(m) for m in mats))
    out = jax.ShapeDtypeStruct(grad_tile.shape, jnp.bfloat16)
    return spectral_call(conv_kernel, out, KS, TILE, args)


def shifted(block, axes, step):
    count = lax.axis_size(axes)
    pairs = [(i, i + step) for i in range(count) if 0 <= i + step < count]
    return lax.ppermute(block, axes, pairs)


def halo(block):
    left, right = shifted(block, COL, 1), shifted(block, COL, -1)
    wide = jnp.concatenate([left, block, right], axis=1)
    low = shifted(wide[-RADIUS:], ROW, 1)
    high = shifted(wide[:RADIUS], ROW, -1)
    return (low, wide, high)


def gelu_parts(values):
    tanh_part = jnp.tanh(root_coef * (values + gelu_coef * values * values * values))
    result = 0.5 * values * (1.0 + tanh_part)
    slopes = 0.5 * (1.0 + tanh_part) + 0.5 * values * (1.0 - tanh_part * tanh_part) * root_coef * (
        1.0 + 3.0 * gelu_coef * values * values
    )
    return (result, slopes)


def to_rows(block):
    rows, cols = block.shape
    return block.reshape(rows // 8, 8, cols // LANES, LANES).transpose(0, 2, 1, 3).reshape(-1, LANES)


def from_rows(flat, shape):
    rows, cols = shape
    return flat.reshape(rows // 8, cols // LANES, 8, LANES).transpose(0, 2, 1, 3).reshape(rows, cols)


def scatter_sum(block, axes):
    count = lax.axis_size(axes)
    parts = block.reshape(count, block.shape[0] // count, LANES)
    arrived = lax.all_to_all(parts, axes, 0, 0)
    return jnp.sum(arrived.astype(jnp.float32), axis=0)


def gathered(block, axes):
    count = lax.axis_size(axes)
    copies = jnp.broadcast_to(block[None], (count,) + block.shape)
    return lax.all_to_all(copies, axes, 0, 0).reshape(count * block.shape[0], LANES)


def summed(dense, taps, scale):
    halves = []
    for blocks in (dense, [taps]):
        flat = jnp.concatenate([to_rows(block.astype(jnp.bfloat16)) for block in blocks], axis=0)
        halves.append(scatter_sum(flat, "core").astype(jnp.bfloat16))
    part = scatter_sum(jnp.concatenate(halves, axis=0), PLANE)
    total = (scatter_sum(part, "z") * scale).astype(jnp.bfloat16)
    both = gathered(gathered(gathered(total, "z"), PLANE), "core").reshape(2, -1, LANES)
    split = halves[0].shape[0]
    return both[:, :split].reshape(-1, LANES), both[:, split:].reshape(-1, LANES)


def block_backward(inputs, stored, upstream, weight_in, weight_out, kernel):
    tile_rows, tile_cols, channels = stored.shape
    flat_z = stored.reshape(tile_rows * tile_cols, channels)
    flat_g = upstream.reshape(tile_rows * tile_cols, channels)
    hidden = jnp.dot(flat_z, weight_in, preferred_element_type=jnp.float32)
    values, slopes = gelu_parts(hidden)
    active = values.astype(jnp.bfloat16)
    back_proj = jnp.einsum("nc,fc->nf", flat_g, weight_out, preferred_element_type=jnp.float32)
    grad_hidden = (back_proj * slopes).astype(jnp.bfloat16)
    grad_flat = (
        flat_g.astype(jnp.float32)
        + jnp.einsum("nf,cf->nc", grad_hidden, weight_in, preferred_element_type=jnp.float32)
    ).astype(jnp.bfloat16)
    sum_in = jnp.einsum("nc,nf->cf", flat_z, grad_hidden, preferred_element_type=jnp.float32)
    sum_out = jnp.einsum("nf,nc->fc", active, flat_g, preferred_element_type=jnp.float32)
    grad_mid = grad_flat.reshape(tile_rows, tile_cols, channels)
    sides_mid = halo(grad_mid)
    tap_sums = taps_gradient(sides_mid, inputs)
    grad_inputs = conv_backward(sides_mid, kernel, grad_mid)
    pixel_count = tile_rows * tile_cols * lax.axis_size(ROW) * lax.axis_size(COL)
    grad_scale = 1.0 / math.sqrt(pixel_count)
    final_dense, final_taps = summed([sum_in, sum_out], tap_sums, grad_scale)
    rows_in = sum_in.size // LANES
    final_in = from_rows(final_dense[:rows_in], sum_in.shape)
    final_out = from_rows(final_dense[rows_in:], sum_out.shape)
    final_kernel = from_rows(final_taps, tap_sums.shape)[: KS * KS].reshape(KS, KS, channels)
    return (grad_inputs, final_in, final_out, final_kernel)


def solution(mesh):
    fine = Mesh(mesh.devices.reshape(2, 4, 2, 2, 16), ("yh", "x", "core", "yl", "z"))
    return jax.shard_map(
        block_backward,
        mesh=fine,
        in_specs=(P(ROW, COL, None), P(ROW, COL, None), P(ROW, COL, None), P(), P(), P()),
        out_specs=(P(ROW, COL, None), P(), P(), P()),
        check_vma=False,
    )
```

```python
import math

import jax
import jax.numpy as jnp
import numpy as np
from jax import lax
from jax.experimental import pallas as pl
from jax.experimental.pallas import tpu as pltpu
from jax.sharding import Mesh, PartitionSpec as P


KS = 27
RADIUS = KS // 2
TILE = 16
PATCH = TILE + KS - 1
HALF = PATCH // 2 + 1
BAND = 24
CELLS = 2 * BAND // 8
ROW = ("yh", "x", "core")
COL = ("yl", "z")
PLANE = ("x", "yh", "yl")
LANES = 128


gelu_coef = 0.044715
root_coef = math.sqrt(2.0 / math.pi)


def split_stack(matrix, order):
    high = matrix.astype(jnp.bfloat16)
    low = (matrix - high.astype(np.float64)).astype(jnp.bfloat16)
    return np.concatenate([{"h": high, "l": low}[part] for part in order], axis=1)


def forward_matrix(positions):
    matrix = np.zeros((2 * BAND, len(positions)))
    freq = np.arange(HALF)
    for column, position in enumerate(positions):
        if position is not None:
            angle = 2.0 * np.pi * ((freq * position) % PATCH) / PATCH
            matrix[:HALF, column] = np.cos(angle)
            matrix[BAND : BAND + HALF, column] = -np.sin(angle)
    return split_stack(matrix, "hl")


def inverse_matrix(positions, rows):
    matrix = np.zeros((rows, 2 * BAND))
    freq = np.arange(HALF)
    weight = np.where((freq == 0) | (2 * freq == PATCH), 1.0, 2.0) / PATCH
    for row, position in enumerate(positions):
        angle = 2.0 * np.pi * ((freq * position) % PATCH) / PATCH
        matrix[row, :HALF] = weight * np.cos(angle)
        matrix[row, BAND : BAND + HALF] = -weight * np.sin(angle)
    return split_stack(matrix, "hlh")


PATCH_POSITIONS = [i - TILE + RADIUS if 0 <= i - TILE + RADIUS < PATCH else None for i in range(3 * TILE)]


def transform(matrix_ref, pixels_ref, out_ref, first, unroll):
    def some(step, carry):
        for extra in range(unroll):
            row = step * unroll + extra
            pixels = jnp.concatenate([pixels_ref[row]] * 2, axis=0)
            spectrum = jnp.dot(matrix_ref[...], pixels, preferred_element_type=jnp.float32)
            for lane in range(2):
                part = spectrum[:, lane * LANES : (lane + 1) * LANES]
                out_ref[first + row, lane * CELLS : (lane + 1) * CELLS] = part.reshape(CELLS, 8, LANES)
        return carry

    lax.fori_loop(0, pixels_ref.shape[0] // unroll, some, 0)


def transform_patch(matrix_ref, core, far, wide, near, out_ref):
    below = RADIUS + TILE
    transform(matrix_ref, far, out_ref, core[0] * below, far.shape[0])
    transform(matrix_ref, wide, out_ref, RADIUS, 8)
    transform(matrix_ref, near, out_ref, (1 - core[0]) * below, near.shape[0])


def back(matrix_ref, spectrum_ref, row):
    lanes = [
        spectrum_ref[row, lane * CELLS : (lane + 1) * CELLS].reshape(2 * BAND, LANES) for lane in range(2)
    ]
    values = jnp.concatenate(lanes, axis=1)
    high = values.astype(jnp.bfloat16)
    low = (values - high.astype(jnp.float32)).astype(jnp.bfloat16)
    stacked = jnp.concatenate([high, high, low], axis=0)
    return jnp.dot(matrix_ref[...], stacked, preferred_element_type=jnp.float32)


def each_cell(work):
    def lane_step(lane, carry):
        def cell_step(cell, inner):
            work(lane * CELLS + cell, lane * CELLS + CELLS // 2 + cell)
            return inner

        return lax.fori_loop(0, CELLS // 2, cell_step, carry)

    lax.fori_loop(0, 2, lane_step, 0)


def taps_kernel(core, far, centre, near, own, patch_mat, tile_mat, inv_mat, out_ref, wide, tile, sums):
    transform(tile_mat, own, tile, 0, 8)
    transform_patch(patch_mat, core, far, centre, near, wide)
    block = 9

    def work(re, im):
        def block_step(index, carry):
            base = index * block
            real = [None] * block
            imag = [None] * block
            for i in range(TILE):
                xr, xi = tile[i, re], tile[i, im]
                for a in range(block):
                    row = i + KS - 1 - base - a
                    gr, gi = wide[row, re], wide[row, im]
                    new_r = xr * gr + xi * gi
                    new_i = xr * gi - xi * gr
                    real[a] = new_r if i == 0 else real[a] + new_r
                    imag[a] = new_i if i == 0 else imag[a] + new_i
            for a in range(block):
                sums[base + a, re] = real[a]
                sums[base + a, im] = imag[a]
            return carry

        lax.fori_loop(0, KS // block, block_step, 0)

    each_cell(work)
    for a in range(KS):
        out_ref[a * KS : (a + 1) * KS, :] = back(inv_mat, sums, a)[:KS]
    out_ref[KS * KS :, :] = jnp.zeros((out_ref.shape[0] - KS * KS, out_ref.shape[1]), jnp.float32)


def conv_kernel(core, far, centre, near, taps, grad, patch_mat, taps_mat, inv_mat, out_ref, wide, filt, sums):
    transform(taps_mat, taps, filt, 0, 9)
    transform_patch(patch_mat, core, far, centre, near, wide)
    block = 8

    def work(re, im):
        def block_step(index, carry):
            base = index * block
            real = [None] * block
            imag = [None] * block
            for a in range(KS):
                kr, ki = filt[a, re], filt[a, im]
                for i in range(block):
                    row = base + i + KS - 1 - a
                    gr, gi = wide[row, re], wide[row, im]
                    new_r = kr * gr - ki * gi
                    new_i = kr * gi + ki * gr
                    real[i] = new_r if a == 0 else real[i] + new_r
                    imag[i] = new_i if a == 0 else imag[i] + new_i
            for i in range(block):
                sums[base + i, re] = real[i]
                sums[base + i, im] = imag[i]
            return carry

        lax.fori_loop(0, TILE // block, block_step, 0)

    each_cell(work)
    for i in range(TILE):
        out_ref[i] = (grad[i].astype(jnp.float32) + back(inv_mat, sums, i)).astype(jnp.bfloat16)


def spectral_call(kernel, out_shape, second_rows, sum_rows, args):
    vmem = pl.BlockSpec(memory_space=pltpu.VMEM)
    return pl.pallas_call(
        kernel,
        out_shape=out_shape,
        in_specs=[pl.BlockSpec(memory_space=pltpu.SMEM)] + [vmem] * (len(args) - 1),
        out_specs=vmem,
        scratch_shapes=[
            pltpu.VMEM((PATCH, 2 * CELLS, 8, LANES), jnp.float32),
            pltpu.VMEM((second_rows, 2 * CELLS, 8, LANES), jnp.float32),
            pltpu.VMEM((sum_rows, 2 * CELLS, 8, LANES), jnp.float32),
        ],
        compiler_params=pltpu.CompilerParams(vmem_limit_bytes=32 << 20),
        cost_estimate=pl.CostEstimate(flops=4_000_000_000, bytes_accessed=8_000_000, transcendentals=0),
    )(*args)


def taps_gradient(sides, own):
    mats = (
        forward_matrix(PATCH_POSITIONS),
        forward_matrix(list(range(TILE))),
        inverse_matrix(range(KS - 1, -1, -1), 32),
    )
    args = (*sides, own, *(jnp.asarray(m) for m in mats))
    out = jax.ShapeDtypeStruct((768, own.shape[-1]), jnp.float32)
    return spectral_call(taps_kernel, out, TILE, KS, args)


def conv_backward(sides, taps, grad_tile):
    mats = (
        forward_matrix(PATCH_POSITIONS),
        forward_matrix(list(range(KS)) + [None] * 5),
        inverse_matrix(range(KS - 1, PATCH), TILE),
    )
    padded = jnp.pad(taps, ((0, 0), (0, 32 - KS), (0, 0)))
    args = (*sides, padded, grad_tile, *(jnp.asarray(m) for m in mats))
    out = jax.ShapeDtypeStruct(grad_tile.shape, jnp.bfloat16)
    return spectral_call(conv_kernel, out, KS, TILE, args)


def shifted(block, axes, step):
    count = lax.axis_size(axes)
    pairs = [(i, i + step) for i in range(count) if 0 <= i + step < count]
    return lax.ppermute(block, axes, pairs)


def swapped(block, axes, first):
    count = lax.axis_size(axes)
    pairs = []
    for i in range(first, count - 1, 2):
        pairs += [(i, i + 1), (i + 1, i)]
    return lax.ppermute(block, axes, pairs)


def halo(block):
    left, right = shifted(block, COL, 1), shifted(block, COL, -1)
    wide = jnp.concatenate([left, block, right], axis=1)
    core = lax.axis_index("core")
    spare = block.shape[0] - RADIUS
    far = swapped(lax.dynamic_slice_in_dim(wide, core * spare, RADIUS, 0), ROW, 1)
    near = swapped(lax.dynamic_slice_in_dim(wide, (1 - core) * spare, RADIUS, 0), ROW, 0)
    return (core.reshape(1), far, wide, near)


def gelu_parts(values):
    tanh_part = jnp.tanh(root_coef * (values + gelu_coef * values * values * values))
    result = 0.5 * values * (1.0 + tanh_part)
    slopes = 0.5 * (1.0 + tanh_part) + 0.5 * values * (1.0 - tanh_part * tanh_part) * root_coef * (
        1.0 + 3.0 * gelu_coef * values * values
    )
    return (result, slopes)


def to_rows(block):
    rows, cols = block.shape
    return block.reshape(rows // 8, 8, cols // LANES, LANES).transpose(0, 2, 1, 3).reshape(-1, LANES)


def from_rows(flat, shape):
    rows, cols = shape
    return flat.reshape(rows // 8, cols // LANES, 8, LANES).transpose(0, 2, 1, 3).reshape(rows, cols)


def scatter_sum(block, axes):
    count = lax.axis_size(axes)
    parts = block.reshape(count, block.shape[0] // count, LANES)
    arrived = lax.all_to_all(parts, axes, 0, 0)
    return jnp.sum(arrived.astype(jnp.float32), axis=0)


def gathered(block, axes):
    count = lax.axis_size(axes)
    copies = jnp.broadcast_to(block[None], (count,) + block.shape)
    return lax.all_to_all(copies, axes, 0, 0).reshape(count * block.shape[0], LANES)


def summed(dense, taps, scale):
    halves = []
    for blocks in (dense, [taps]):
        flat = jnp.concatenate([to_rows(block.astype(jnp.bfloat16)) for block in blocks], axis=0)
        halves.append(scatter_sum(flat, "core").astype(jnp.bfloat16))
    part = scatter_sum(jnp.concatenate(halves, axis=0), PLANE)
    total = (scatter_sum(part, "z") * scale).astype(jnp.bfloat16)
    run = gathered(total, "z")
    own = gathered(run, PLANE)
    other = swapped(own, ROW, 0)
    first = lax.axis_index("core") == 0
    pair = (jnp.where(first, own, other), jnp.where(first, other, own))
    split = halves[0].shape[0]
    return [jnp.concatenate([half[rows] for half in pair], axis=0) for rows in (slice(0, split), slice(split, None))]


def block_backward(inputs, stored, upstream, weight_in, weight_out, kernel):
    tile_rows, tile_cols, channels = stored.shape
    flat_z = stored.reshape(tile_rows * tile_cols, channels)
    flat_g = upstream.reshape(tile_rows * tile_cols, channels)
    hidden = jnp.dot(flat_z, weight_in, preferred_element_type=jnp.float32)
    values, slopes = gelu_parts(hidden)
    active = values.astype(jnp.bfloat16)
    back_proj = jnp.einsum("nc,fc->nf", flat_g, weight_out, preferred_element_type=jnp.float32)
    grad_hidden = (back_proj * slopes).astype(jnp.bfloat16)
    grad_flat = (
        flat_g.astype(jnp.float32)
        + jnp.einsum("nf,cf->nc", grad_hidden, weight_in, preferred_element_type=jnp.float32)
    ).astype(jnp.bfloat16)
    sum_in = jnp.einsum("nc,nf->cf", flat_z, grad_hidden, preferred_element_type=jnp.float32)
    sum_out = jnp.einsum("nf,nc->fc", active, flat_g, preferred_element_type=jnp.float32)
    grad_mid = grad_flat.reshape(tile_rows, tile_cols, channels)
    sides_mid = halo(grad_mid)
    tap_sums = taps_gradient(sides_mid, inputs)
    grad_inputs = conv_backward(sides_mid, kernel, grad_mid)
    pixel_count = tile_rows * tile_cols * lax.axis_size(ROW) * lax.axis_size(COL)
    grad_scale = 1.0 / math.sqrt(pixel_count)
    final_dense, final_taps = summed([sum_in, sum_out], tap_sums, grad_scale)
    rows_in = sum_in.size // LANES
    final_in = from_rows(final_dense[:rows_in], sum_in.shape)
    final_out = from_rows(final_dense[rows_in:], sum_out.shape)
    final_kernel = from_rows(final_taps, tap_sums.shape)[: KS * KS].reshape(KS, KS, channels)
    return (grad_inputs, final_in, final_out, final_kernel)


def solution(mesh):
    fine = Mesh(mesh.devices.reshape(2, 4, 2, 2, 16), ("yh", "x", "core", "yl", "z"))
    return jax.shard_map(
        block_backward,
        mesh=fine,
        in_specs=(P(ROW, COL, None), P(ROW, COL, None), P(ROW, COL, None), P(), P(), P()),
        out_specs=(P(ROW, COL, None), P(), P(), P()),
        check_vma=False,
    )
```
